512 devices in a mesh: band: 64 (over x, y, z_hi), pw: 8 (over z_lo, core).
Axes of the slice: x: 4, y: 8, z: 8 (z_hi: 2, z_lo: 4; z = z_hi * 4 + z_lo), core: 2. Of those that a mesh axis runs over, the one named last changes fastest.
Arguments:
- occupied: bfloat16 [2, 64, 4096], P(None, 'pw'), may hold values from -6 to 6
- virtual: bfloat16 [64, 64, 4096], P('band', 'pw'), may hold values from -6 to 6
- screening: bfloat16 [16384, 16384], P('pw', 'band'), may hold values from -0.046875 to 0.046875
- grid_index: int32 [16384], replicated, may hold values from 0 to 262143, as said below
Outputs:
- grad_vir: float32 [64, 64, 4096], P('band', 'pw')
The draws below stay inside these ranges and needn't reach their ends.
Inputs may be any that keep to these rules, and one draw needn't show every extreme that they name: `grid_index`: all entries are distinct. Write each entry as (kx * 64 + ky) * 64 + kz and take kx, ky, kz as signed frequencies (a value k of 32 or more stands for k - 64): every signed frequency lies within -16 to 16, and some entry has |kx| = |ky| = |kz| = 16. The entries g with g // 2048 = b are grid points whose ky is congruent to b modulo 64 // 8.
All inputs are finite; a program needn't handle non-finite values.
Results may differ from the reference program's by a relative error of at most 0.006.
Values may be sent and summed in bfloat16 or wider, within the bound.
A program may use at most 128 MiB of HBM per device.

```python
import jax
import jax.numpy as jnp
from jax import lax

GRID = 64
NG = 16384
OCC_WIN = 2
NVIR = 64
BLOCK_G = 2048
SLAB_ROWS = 8
KMAX = 16


def wrapped(freq):
    return jnp.where(freq >= GRID // 2, freq - GRID, freq)


def draw_grid_index(key, part):
    class_count = GRID // SLAB_ROWS
    cells = jnp.arange(GRID ** 3, dtype=jnp.int32)
    freq_x = jnp.abs(wrapped(cells // (GRID * GRID)))
    freq_y = jnp.abs(wrapped(cells // GRID % GRID))
    freq_z = jnp.abs(wrapped(cells % GRID))
    class_of = cells // GRID % GRID % class_count
    inside = (freq_x <= KMAX) & (freq_y <= KMAX) & (freq_z <= KMAX)
    corner = (freq_x == KMAX) & (freq_y == KMAX) & (freq_z == KMAX)
    priority = jnp.where(corner, 0, jnp.where(inside, 1, 2)).astype(jnp.int32)
    jitter = jax.random.randint(jax.random.fold_in(key, 11), (GRID ** 3,), 0, 4096).astype(jnp.int32)
    jitter = jitter * GRID ** 3 + cells
    shuffled = jnp.argsort(jitter, stable=True).astype(jnp.int32)
    primary = (class_of * 3 + priority)[shuffled]
    second = jnp.argsort(primary, stable=True).astype(jnp.int32)
    order = shuffled[second]
    picked = order.reshape(class_count, GRID ** 3 // class_count)[:, :BLOCK_G]
    return picked.reshape(-1).astype(jnp.int32)


def block_scale(own_key, dims, pieces, least, high):
    loudness = 1.0
    for axis_at, shards_of in pieces:
        draws = jax.random.uniform(jax.random.fold_in(jax.random.fold_in(own_key, 6), axis_at), (shards_of,), jnp.float32, least / len(pieces), high / len(pieces))
        loudness = loudness * jnp.repeat(jnp.exp(draws), dims[axis_at] // shards_of).reshape((-1,) + (1,) * (len(dims) - 1 - axis_at))
    return loudness


def bell_draw(stream_key, extent, width, most, shards=(), kind=jnp.bfloat16):
    result = width * jax.random.normal(stream_key, extent, jnp.float32)
    if shards:
        result = result * block_scale(stream_key, extent, shards, -0.22, 0.18)
    return jnp.clip(result, -most, most).astype(kind)


def setup_inputs(seed: int = 0) -> dict:
    streams_of = jax.random.split(jax.random.key(seed), 5)
    return {
        "occupied": bell_draw(streams_of[0], (OCC_WIN, GRID, GRID * GRID), 1.0, 6.0, ((1, 8),)),
        "virtual": bell_draw(streams_of[1], (NVIR, GRID, GRID * GRID), 1.0, 6.0, ((0, 64), (1, 8))),
        "screening": bell_draw(streams_of[2], (NG, NG), NG ** -0.5, 0.046875, ((0, 8), (1, 64))),
        "grid_index": draw_grid_index(jax.random.fold_in(streams_of[4], 71), 0),
    }


def reference(occupied, virtual, screening, grid_index):
    occ_full = occupied.astype(jnp.float32).reshape(-1, GRID, GRID, GRID)
    vir_full = virtual.astype(jnp.float32).reshape(-1, GRID, GRID, GRID)
    norm_in = 1.0 / (float(GRID) ** 1.5)
    norm_out = float(GRID) ** 3 / (float(NG) ** 0.5)

    def forward_one(orbital):
        products = occ_full * orbital[None]
        eigen_spectrum = jnp.fft.fftn(products, axes=(1, 2, 3)).reshape(occ_full.shape[0], -1)
        picked = eigen_spectrum[:, grid_index]
        return jnp.stack([jnp.real(picked), jnp.imag(picked)], axis=1) * norm_in

    eigen_spectra = lax.map(forward_one, vir_full).astype(jnp.bfloat16)
    flat_rows = eigen_spectra.reshape(-1, NG)
    screened = jnp.dot(flat_rows, screening, preferred_element_type=jnp.float32).astype(jnp.bfloat16)
    screened = screened.reshape(eigen_spectra.shape).astype(jnp.float32)

    def back_one(values):
        empty_grid = jnp.zeros((values.shape[0], GRID ** 3), values.dtype)
        real_grid = empty_grid.at[:, grid_index].set(values[:, 0])
        imag_grid = empty_grid.at[:, grid_index].set(values[:, 1])
        eigen_spectrum = (real_grid + 1j * imag_grid).reshape(-1, GRID, GRID, GRID)
        screened_potential = jnp.real(jnp.fft.ifftn(eigen_spectrum, axes=(1, 2, 3))) * norm_out
        return jnp.sum(screened_potential * occ_full, axis=0)

    gradient = lax.map(back_one, screened)
    return gradient.reshape(-1, GRID, GRID * GRID)
```

```python
import math

import jax
import jax.numpy as jnp
from jax import lax
from jax.sharding import PartitionSpec as P

GRID = 64
NG = 16384
KMAX = 16
NK = 2 * KMAX + 1
PW = 8
BAND = 64
NJ = 5
PRECISE = lax.Precision.HIGHEST
F32 = jnp.float32
BF16 = jnp.bfloat16


def phases(left, right):
    angles = (left[:, None] * right[None, :] % GRID).astype(F32) * (2.0 * math.pi / GRID)
    return jnp.cos(angles), jnp.sin(angles)


def dot(spec, a, b):
    return jnp.einsum(spec, a, b, precision=PRECISE, preferred_element_type=F32)


def body(occupied, virtual, screening, grid_index):
    pairs, planes = occupied.shape[0], occupied.shape[1]
    slab = lax.axis_index("pw")
    cells = jnp.arange(GRID, dtype=jnp.int32)
    freqs = jnp.arange(NK, dtype=jnp.int32) - KMAX
    row_freqs = jnp.arange(PW, dtype=jnp.int32)[:, None] - KMAX + PW * jnp.arange(NJ, dtype=jnp.int32)[None]
    cos_k, sin_k = phases(cells, freqs)
    cos_y, sin_y = phases(cells, row_freqs.reshape(-1))

    block = NG // PW
    own = lax.dynamic_slice_in_dim(grid_index, slab * block, block)

    def signed(k):
        return jnp.where(k >= GRID // 2, k - GRID, k)

    at_x = signed(own // (GRID * GRID)) + KMAX
    at_j = (signed(own // GRID % GRID) + KMAX - slab) // PW
    at_z = signed(own % GRID) + KMAX
    at_jz = at_j * NK + at_z
    pick_x = (jnp.arange(NK, dtype=jnp.int32)[:, None] == at_x[None]).astype(BF16)
    pick_jz = jnp.arange(NJ * NK, dtype=jnp.int32)[:, None] == at_jz[None]

    density = occupied.astype(F32) * virtual.astype(F32)
    density = density.reshape(pairs, planes, GRID, GRID)
    forward_z = jnp.concatenate([cos_k, -sin_k], axis=1)
    field = dot("pxyz,zc->pxyc", density, forward_z)
    both_y = jnp.concatenate([cos_y, sin_y], axis=1)
    mixed = dot("pxyc,yk->pxkc", field, both_y).reshape(pairs, planes, 2, PW, NJ, 2, NK)
    real = mixed[:, :, 0, :, :, 0] + mixed[:, :, 1, :, :, 1]
    imag = mixed[:, :, 0, :, :, 1] - mixed[:, :, 1, :, :, 0]
    field = jnp.stack([real, imag], axis=0).astype(BF16)
    field = field.transpose(3, 2, 1, 0, 4, 5).reshape(PW, planes, pairs * 2 * NJ * NK)
    pencil = lax.all_to_all(field, "pw", 0, 0, tiled=True).reshape(GRID, -1)

    cos_sin = jnp.concatenate([cos_k, sin_k], axis=1)
    mixed = dot("xm,xk->mk", pencil.astype(F32), cos_sin).reshape(pairs, 2, NJ * NK, 2, NK)
    real = mixed[:, 0, :, 0] + mixed[:, 1, :, 1]
    imag = mixed[:, 1, :, 0] - mixed[:, 0, :, 1]
    box = (jnp.stack([real, imag], axis=1) * (1.0 / math.sqrt(GRID**3))).astype(BF16)
    columns = jnp.einsum("prmk,kg->prmg", box, pick_x, preferred_element_type=F32)
    spectra = jnp.sum(jnp.where(pick_jz[None, None], columns, 0.0), axis=2).astype(BF16)

    rows = pairs * 2
    everyone = lax.all_gather(spectra.reshape(rows, block), "band", axis=0, tiled=True)
    partial = jnp.dot(everyone, screening, preferred_element_type=F32).astype(BF16)

    width = screening.shape[1]
    partial = lax.all_to_all(partial.reshape(PW, PW * rows, width), "pw", 0, 0, tiled=True)
    summed = jnp.sum(partial.astype(F32), axis=0).astype(BF16).reshape(PW, rows, width)
    turn = []
    for c1 in range(PW):
        for c0 in range(PW):
            for p in range(PW):
                turn.append(((c1 * PW + c0) * PW + p, (p * PW + c0) * PW + c1))
    summed = lax.ppermute(summed, ("band", "pw"), turn)
    groups = [[PW * k + t for t in range(PW)] for k in range(BAND // PW)]
    home = lax.all_to_all(summed, "band", 0, 0, axis_index_groups=groups, tiled=True)
    screened = home.transpose(1, 0, 2).reshape(rows, 1, block)

    spread = jnp.where(pick_jz[None], screened, jnp.zeros((), BF16)).reshape(rows * NJ * NK, block)
    box = jnp.einsum("mg,kg->mk", spread, pick_x, preferred_element_type=F32)
    mixed = dot("xk,mk->xm", jnp.concatenate([cos_k, sin_k], axis=0), box)
    mixed = mixed.reshape(2, GRID, pairs, 2, NJ * NK)
    real = mixed[0, :, :, 0] - mixed[1, :, :, 1]
    imag = mixed[0, :, :, 1] + mixed[1, :, :, 0]
    pencil = jnp.stack([real, imag], axis=2).astype(BF16).reshape(PW, planes, -1)
    field = lax.all_to_all(pencil, "pw", 0, 0, tiled=True)
    field = field.reshape(PW, planes, pairs, 2, NJ, NK).astype(F32)
    field = field.transpose(2, 1, 0, 4, 3, 5).reshape(pairs, planes, PW * NJ, 2 * NK)
    mixed = dot("pxkc,yk->pxyc", field, jnp.concatenate([cos_y, sin_y], axis=0))
    mixed = mixed.reshape(pairs, planes, 2, GRID, 2 * NK)
    mixed = jnp.concatenate([mixed[:, :, 0], mixed[:, :, 1]], axis=-1)
    cz, sz = jnp.transpose(cos_k), jnp.transpose(sin_k)
    back = jnp.concatenate([cz, -sz, -sz, -cz], axis=0) * (1.0 / math.sqrt(NG))
    potential = dot("pxyc,cz->pxyz", mixed, back)
    weighted = potential.reshape(pairs, planes, GRID * GRID) * occupied.astype(F32)
    return jnp.sum(weighted, axis=0)[None]


def solution(mesh):
    return jax.shard_map(
        body,
        mesh=mesh,
        in_specs=(P(None, "pw", None), P("band", "pw", None), P("pw", "band"), P()),
        out_specs=P("band", "pw", None),
        check_vma=False,
    )
```

```python
import math

import jax
import jax.numpy as jnp
from jax import lax
from jax.experimental import pallas as pl
from jax.experimental.pallas import tpu as pltpu
from jax.sharding import PartitionSpec as P

GRID = 64
NG = 16384
KMAX = 16
NK = 2 * KMAX + 1
PW = 8
BAND = 64
NJ = 5
PRECISE = lax.Precision.HIGHEST
F32 = jnp.float32
BF16 = jnp.bfloat16


def phases(left, right):
    angles = (left[:, None] * right[None, :] % GRID).astype(F32) * (2.0 * math.pi / GRID)
    return jnp.cos(angles), jnp.sin(angles)


def dot(spec, a, b):
    return jnp.einsum(spec, a, b, precision=PRECISE, preferred_element_type=F32)


MESH = pl.DeviceIdType.MESH


def remote(src, dst, send, recv, device):
    return pltpu.make_async_remote_copy(
        src_ref=src, dst_ref=dst, send_sem=send, recv_sem=recv, device_id=device, device_id_type=MESH
    )


def greet(devices, count):
    barrier = pltpu.get_barrier_semaphore()
    for device in devices:
        pl.semaphore_signal(barrier, inc=1, device_id=device, device_id_type=MESH)
    pl.semaphore_wait(barrier, count)


OFFSETS = (1, 7, 2, 6, 3, 5, 4)


def gather_kernel(own_ref, all_ref, own_sem, z_sems, ys_sems, yr_sems, xs_sems, xr_sems, fs_sems, fr_sems):
    band, pw = lax.axis_index("band"), lax.axis_index("pw")
    x, y, z = band // 16, lax.rem(band // 2, 8), lax.rem(band, 2)

    def at(x_at, y_at, z_at):
        return (x_at * 16 + y_at * 2 + z_at, pw)

    def up(d):
        return lax.rem(y + d, 8)

    right, left = lax.rem(x + 1, 4), lax.rem(x + 3, 4)
    across = at(x, y, 1 - z)
    beside = (at(right, y, z), at(left, y, z))
    greet([across, *beside, *[at(x, up(d), z) for d in OFFSETS]], 3 + len(OFFSETS))

    keep = pltpu.make_async_copy(own_ref, all_ref.at[x, y, z], own_sem)
    keep.start()
    to_across = remote(own_ref, all_ref.at[x, y, z], z_sems.at[0], z_sems.at[1], across)
    to_across.start()
    y_copies = {}
    for d in OFFSETS:
        y_copies[0, d] = remote(
            own_ref, all_ref.at[x, y, z], ys_sems.at[0, d], yr_sems.at[0, d], at(x, up(d), z)
        )
        y_copies[0, d].start()
    to_across.wait_recv()
    other = all_ref.at[x, y, 1 - z]
    for d in OFFSETS:
        y_copies[1, d] = remote(other, other, ys_sems.at[1, d], yr_sems.at[1, d], at(x, up(d), z))
        y_copies[1, d].start()
    keep.wait()
    order = (0,) + OFFSETS
    x_copies = []
    for k, d in enumerate(order):
        if d:
            y_copies[0, d].wait_recv()
            y_copies[1, d].wait_recv()
        piece = all_ref.at[x, lax.rem(y + 8 - d, 8)]
        for side in range(2):
            copy = remote(piece, piece, xs_sems.at[side, k], xr_sems.at[side, k], beside[side])
            copy.start()
            x_copies.append(copy)
    forwards = []
    for k, d in enumerate(order):
        first = k % 2
        for side in (first, 1 - first):
            x_copies[2 * k + side].wait_recv()
            if side == first:
                source = left if side == 0 else right
                piece = all_ref.at[source, lax.rem(y + 8 - d, 8)]
                copy = remote(piece, piece, fs_sems.at[k], fr_sems.at[k], beside[side])
                copy.start()
                forwards.append(copy)
    for copy in forwards:
        copy.wait_recv()
    to_across.wait_send()
    for copy in [*y_copies.values(), *x_copies, *forwards]:
        copy.wait_send()


def gathered(own):
    dma = pltpu.SemaphoreType.DMA
    return pl.pallas_call(
        gather_kernel,
        out_shape=jax.ShapeDtypeStruct((4, 8, 2, *own.shape), own.dtype),
        in_specs=[pl.BlockSpec(memory_space=pltpu.VMEM)],
        out_specs=pl.BlockSpec(memory_space=pltpu.VMEM),
        scratch_shapes=[
            dma, dma((2,)), dma((2, 8)), dma((2, 8)), dma((2, 8)), dma((2, 8)), dma((8,)), dma((8,))
        ],
        compiler_params=pltpu.CompilerParams(collective_id=0, has_side_effects=True),
    )(own)


def home_kernel(part_ref, home_ref, landed, summed, ps_sems, pr_sems, cs_sems, cr_sems, own_sem):
    band, pw = lax.axis_index("band"), lax.axis_index("pw")
    high, low = band // PW, lax.rem(band, PW)
    same = high == pw

    def over(d):
        return lax.rem(pw + d, PW)

    barrier = pltpu.get_barrier_semaphore()
    for d in range(1, PW):
        pl.semaphore_signal(barrier, inc=1, device_id=(band, over(d)), device_id_type=MESH)
    for t in range(PW):
        @pl.when(jnp.logical_not(same & (low == t)))
        def _():
            pl.semaphore_signal(barrier, inc=1, device_id=(pw * PW + t, high), device_id_type=MESH)
    pl.semaphore_wait(barrier, jnp.where(same, 2 * PW - 2, 2 * PW - 1))

    copies = []
    for d in range(1, PW):
        copy = remote(part_ref.at[over(d)], landed.at[pw], ps_sems.at[d], pr_sems.at[d], (band, over(d)))
        copy.start()
        copies.append(copy)
    total = part_ref[pw].astype(F32)
    for d in range(1, PW):
        copies[d - 1].wait_recv()
        total = total + landed[lax.rem(pw + PW - d, PW)].astype(F32)
    rows = total.shape[0] // PW
    for t in range(PW):
        summed[t] = total[t * rows : (t + 1) * rows]

    def across(t, sem):
        return remote(summed.at[t], home_ref.at[low], cs_sems.at[t], cr_sems.at[sem], (pw * PW + t, high))

    for t in range(PW):
        mine = same & (low == t)

        @pl.when(mine)
        def _():
            own = pltpu.make_async_copy(summed.at[t], home_ref.at[low], own_sem)
            own.start()
            own.wait()

        @pl.when(jnp.logical_not(mine))
        def _():
            across(t, low).start()

    for t in range(PW):
        @pl.when(jnp.logical_not(same & (low == t)))
        def _():
            pltpu.make_async_remote_copy(
                src_ref=summed.at[t], dst_ref=home_ref.at[t], send_sem=cs_sems.at[t],
                recv_sem=cr_sems.at[t], device_id=(pw * PW + t, high), device_id_type=MESH,
            ).wait()
    for copy in copies:
        copy.wait_send()


def brought_home(partial):
    dma = pltpu.SemaphoreType.DMA
    rows, width = partial.shape[1] // PW, partial.shape[2]
    return pl.pallas_call(
        home_kernel,
        out_shape=jax.ShapeDtypeStruct((PW, rows, width), F32),
        in_specs=[pl.BlockSpec(memory_space=pltpu.VMEM)],
        out_specs=pl.BlockSpec(memory_space=pltpu.VMEM),
        scratch_shapes=[
            pltpu.VMEM(partial.shape, BF16), pltpu.VMEM((PW, rows, width), F32),
            dma((PW,)), dma((PW,)), dma((PW,)), dma((PW,)), dma,
        ],
        compiler_params=pltpu.CompilerParams(collective_id=1, has_side_effects=True),
    )(partial)


def body(occupied, virtual, screening, grid_index):
    pairs, planes = occupied.shape[0], occupied.shape[1]
    slab = lax.axis_index("pw")
    cells = jnp.arange(GRID, dtype=jnp.int32)
    freqs = jnp.arange(NK, dtype=jnp.int32) - KMAX
    row_freqs = jnp.arange(PW, dtype=jnp.int32)[:, None] - KMAX + PW * jnp.arange(NJ, dtype=jnp.int32)[None]
    cos_k, sin_k = phases(cells, freqs)
    cos_y, sin_y = phases(cells, row_freqs.reshape(-1))

    block = NG // PW
    own = lax.dynamic_slice_in_dim(grid_index, slab * block, block)

    def signed(k):
        return jnp.where(k >= GRID // 2, k - GRID, k)

    at_x = signed(own // (GRID * GRID)) + KMAX
    at_j = (signed(own // GRID % GRID) + KMAX - slab) // PW
    at_z = signed(own % GRID) + KMAX
    at_jz = at_j * NK + at_z
    pick_x = (jnp.arange(NK, dtype=jnp.int32)[:, None] == at_x[None]).astype(BF16)
    pick_jz = jnp.arange(NJ * NK, dtype=jnp.int32)[:, None] == at_jz[None]

    density = occupied.astype(F32) * virtual.astype(F32)
    density = density.reshape(pairs, planes, GRID, GRID)
    forward_z = jnp.concatenate([cos_k, -sin_k], axis=1)
    field = dot("pxyz,zc->pxyc", density, forward_z)
    both_y = jnp.concatenate([cos_y, sin_y], axis=1)
    mixed = dot("pxyc,yk->pxkc", field, both_y).reshape(pairs, planes, 2, PW, NJ, 2, NK)
    real = mixed[:, :, 0, :, :, 0] + mixed[:, :, 1, :, :, 1]
    imag = mixed[:, :, 0, :, :, 1] - mixed[:, :, 1, :, :, 0]
    field = jnp.stack([real, imag], axis=0).astype(BF16)
    field = field.transpose(3, 2, 1, 0, 4, 5).reshape(PW, planes, pairs * 2 * NJ * NK)
    pencil = lax.all_to_all(field, "pw", 0, 0, tiled=True).reshape(GRID, -1)

    cos_sin = jnp.concatenate([cos_k, sin_k], axis=1)
    mixed = dot("xm,xk->mk", pencil.astype(F32), cos_sin).reshape(pairs, 2, NJ * NK, 2, NK)
    real = mixed[:, 0, :, 0] + mixed[:, 1, :, 1]
    imag = mixed[:, 1, :, 0] - mixed[:, 0, :, 1]
    box = (jnp.stack([real, imag], axis=1) * (1.0 / math.sqrt(GRID**3))).astype(BF16)
    columns = jnp.einsum("prmk,mg->prkg", box, pick_jz.astype(BF16), preferred_element_type=F32)
    spectra = jnp.sum(columns * pick_x.astype(F32), axis=2).astype(BF16)

    rows = pairs * 2
    everyone = gathered(spectra.reshape(rows, block)).reshape(BAND * rows, block)
    partial = jnp.dot(everyone, screening, preferred_element_type=F32).astype(BF16)

    width = screening.shape[1]
    home = brought_home(partial.reshape(PW, PW * rows, width)).astype(BF16)
    screened = home.transpose(1, 0, 2).reshape(rows, 1, block)

    spread = (screened * pick_x[None]).reshape(rows * NK, block)
    box = jnp.einsum("mg,kg->mk", pick_jz.astype(BF16), spread, preferred_element_type=F32)
    box = box.reshape(NJ * NK, rows, NK)
    mixed = dot("xk,mqk->xqm", jnp.concatenate([cos_k, sin_k], axis=0), box)
    mixed = mixed.reshape(2, GRID, pairs, 2, NJ * NK)
    real = mixed[0, :, :, 0] - mixed[1, :, :, 1]
    imag = mixed[0, :, :, 1] + mixed[1, :, :, 0]
    pencil = jnp.stack([real, imag], axis=2).astype(BF16).reshape(PW, planes, -1)
    field = lax.all_to_all(pencil, "pw", 0, 0, tiled=True)
    field = field.reshape(PW, planes, pairs, 2, NJ, NK).astype(F32)
    field = field.transpose(2, 1, 0, 4, 3, 5).reshape(pairs, planes, PW * NJ, 2 * NK)
    mixed = dot("pxkc,yk->pxyc", field, jnp.concatenate([cos_y, sin_y], axis=0))
    mixed = mixed.reshape(pairs, planes, 2, GRID, 2 * NK)
    mixed = jnp.concatenate([mixed[:, :, 0], mixed[:, :, 1]], axis=-1)
    cz, sz = jnp.transpose(cos_k), jnp.transpose(sin_k)
    back = jnp.concatenate([cz, -sz, -sz, -cz], axis=0) * (1.0 / math.sqrt(NG))
    potential = dot("pxyc,cz->pxyz", mixed, back)
    weighted = potential.reshape(pairs, planes, GRID * GRID) * occupied.astype(F32)
    return jnp.sum(weighted, axis=0)[None]


def solution(mesh):
    return jax.shard_map(
        body,
        mesh=mesh,
        in_specs=(P(None, "pw", None), P("band", "pw", None), P("pw", "band"), P()),
        out_specs=P("band", "pw", None),
        check_vma=False,
    )
```

```python
import math

import jax
import jax.numpy as jnp
from jax import lax
from jax.experimental import pallas as pl
from jax.experimental.pallas import tpu as pltpu
from jax.sharding import PartitionSpec as P

GRID = 64
NG = 16384
KMAX = 16
NK = 2 * KMAX + 1
PW = 8
BAND = 64
NJ = 5
PRECISE = lax.Precision.HIGHEST
F32 = jnp.float32
BF16 = jnp.bfloat16


def phases(left, right):
    angles = (left[:, None] * right[None, :] % GRID).astype(F32) * (2.0 * math.pi / GRID)
    return jnp.cos(angles), jnp.sin(angles)


def dot(spec, a, b):
    return jnp.einsum(spec, a, b, precision=PRECISE, preferred_element_type=F32)


MESH = pl.DeviceIdType.MESH


def remote(src, dst, send, recv, device):
    return pltpu.make_async_remote_copy(
        src_ref=src, dst_ref=dst, send_sem=send, recv_sem=recv, device_id=device, device_id_type=MESH
    )


OFFSETS = (1, 7, 2, 6, 3, 5, 4)


def screen_kernel(
    own_ref, screening_ref, home_ref, all_ref, part_ref, landed, summed, own_sem, z_sems, ys_sems,
    yr_sems, xs_sems, xr_sems, fs_sems, fr_sems, ps_sems, pr_sems, cs_sems, cr_sems
):
    band, pw = lax.axis_index("band"), lax.axis_index("pw")
    x, y, z = band // 16, lax.rem(band // 2, 8), lax.rem(band, 2)

    def at(x_at, y_at, z_at):
        return (x_at * 16 + y_at * 2 + z_at, pw)

    def up(d):
        return lax.rem(y + d, 8)

    right, left = lax.rem(x + 1, 4), lax.rem(x + 3, 4)
    across = at(x, y, 1 - z)
    beside = (at(right, y, z), at(left, y, z))
    high, low = band // PW, lax.rem(band, PW)
    same = high == pw

    def over(d):
        return lax.rem(pw + d, PW)

    barrier = pltpu.get_barrier_semaphore()
    for t in range(PW):
        @pl.when(jnp.logical_not(same & (low == t)))
        def _():
            pl.semaphore_signal(barrier, inc=1, device_id=(pw * PW + t, high), device_id_type=MESH)
    near = [across, *beside, *[at(x, up(d), z) for d in OFFSETS], *[(band, over(d)) for d in range(1, PW)]]
    for device in near:
        pl.semaphore_signal(barrier, inc=1, device_id=device, device_id_type=MESH)
    pl.semaphore_wait(barrier, len(near) + PW - jnp.where(same, 1, 0))

    keep = pltpu.make_async_copy(own_ref, all_ref.at[x, y, z], own_sem)
    keep.start()
    to_across = remote(own_ref, all_ref.at[x, y, z], z_sems.at[0], z_sems.at[1], across)
    to_across.start()
    y_copies = {}
    for d in OFFSETS:
        y_copies[0, d] = remote(
            own_ref, all_ref.at[x, y, z], ys_sems.at[0, d], yr_sems.at[0, d], at(x, up(d), z)
        )
        y_copies[0, d].start()
    to_across.wait_recv()
    other = all_ref.at[x, y, 1 - z]
    for d in OFFSETS:
        y_copies[1, d] = remote(other, other, ys_sems.at[1, d], yr_sems.at[1, d], at(x, up(d), z))
        y_copies[1, d].start()
    keep.wait()
    order = (0,) + OFFSETS
    x_copies = []
    for k, d in enumerate(order):
        if d:
            y_copies[0, d].wait_recv()
            y_copies[1, d].wait_recv()
        piece = all_ref.at[x, lax.rem(y + 8 - d, 8)]
        for side in range(2):
            copy = remote(piece, piece, xs_sems.at[side, k], xr_sems.at[side, k], beside[side])
            copy.start()
            x_copies.append(copy)
    forwards = []
    for k, d in enumerate(order):
        first = k % 2
        for side in (first, 1 - first):
            x_copies[2 * k + side].wait_recv()
            if side == first:
                source = left if side == 0 else right
                piece = all_ref.at[source, lax.rem(y + 8 - d, 8)]
                copy = remote(piece, piece, fs_sems.at[k], fr_sems.at[k], beside[side])
                copy.start()
                forwards.append(copy)
    for copy in forwards:
        copy.wait_recv()
    rows = all_ref.shape[3]
    everyone = all_ref[...].reshape(BAND * rows, all_ref.shape[4])
    partial = jnp.dot(everyone, screening_ref[...], preferred_element_type=F32).astype(BF16)
    part_ref[...] = partial.reshape(part_ref.shape)

    copies = []
    for d in range(1, PW):
        copy = remote(part_ref.at[over(d)], landed.at[pw], ps_sems.at[d], pr_sems.at[d], (band, over(d)))
        copy.start()
        copies.append(copy)
    total = part_ref[pw].astype(F32)
    for d in range(1, PW):
        copies[d - 1].wait_recv()
        total = total + landed[lax.rem(pw + PW - d, PW)].astype(F32)
    for t in range(PW):
        summed[t] = total[t * rows : (t + 1) * rows]

    def send_home(t, sem):
        return remote(summed.at[t], home_ref.at[low], cs_sems.at[t], cr_sems.at[sem], (pw * PW + t, high))

    for t in range(PW):
        mine = same & (low == t)

        @pl.when(mine)
        def _():
            own = pltpu.make_async_copy(summed.at[t], home_ref.at[low], own_sem)
            own.start()
            own.wait()

        @pl.when(jnp.logical_not(mine))
        def _():
            send_home(t, low).start()

    for t in range(PW):
        @pl.when(jnp.logical_not(same & (low == t)))
        def _():
            pltpu.make_async_remote_copy(
                src_ref=summed.at[t], dst_ref=home_ref.at[t], send_sem=cs_sems.at[t],
                recv_sem=cr_sems.at[t], device_id=(pw * PW + t, high), device_id_type=MESH,
            ).wait()
    for copy in copies:
        copy.wait_send()
    to_across.wait_send()
    for copy in [*y_copies.values(), *x_copies, *forwards]:
        copy.wait_send()


def screened_home(own, screening):
    dma = pltpu.SemaphoreType.DMA
    rows, width = own.shape[0], screening.shape[1]
    return pl.pallas_call(
        screen_kernel,
        out_shape=jax.ShapeDtypeStruct((PW, rows, width), F32),
        in_specs=[pl.BlockSpec(memory_space=pltpu.VMEM)] * 2,
        out_specs=pl.BlockSpec(memory_space=pltpu.VMEM),
        scratch_shapes=[
            pltpu.VMEM((4, 8, 2, *own.shape), BF16),
            pltpu.VMEM((PW, PW * rows, width), BF16),
            pltpu.VMEM((PW, PW * rows, width), BF16),
            pltpu.VMEM((PW, rows, width), F32),
            dma, dma((2,)), dma((2, 8)), dma((2, 8)), dma((2, 8)), dma((2, 8)), dma((8,)), dma((8,)),
            dma((PW,)), dma((PW,)), dma((PW,)), dma((PW,)),
        ],
        compiler_params=pltpu.CompilerParams(collective_id=0, has_side_effects=True),
    )(own, screening)


def body(occupied, virtual, screening, grid_index):
    pairs, planes = occupied.shape[0], occupied.shape[1]
    slab = lax.axis_index("pw")
    cells = jnp.arange(GRID, dtype=jnp.int32)
    freqs = jnp.arange(NK, dtype=jnp.int32) - KMAX
    row_freqs = jnp.arange(PW, dtype=jnp.int32)[:, None] - KMAX + PW * jnp.arange(NJ, dtype=jnp.int32)[None]
    cos_k, sin_k = phases(cells, freqs)
    cos_y, sin_y = phases(cells, row_freqs.reshape(-1))

    block = NG // PW
    own = lax.dynamic_slice_in_dim(grid_index, slab * block, block)

    def signed(k):
        return jnp.where(k >= GRID // 2, k - GRID, k)

    at_x = signed(own // (GRID * GRID)) + KMAX
    at_j = (signed(own // GRID % GRID) + KMAX - slab) // PW
    at_z = signed(own % GRID) + KMAX
    at_jz = at_j * NK + at_z
    pick_x = (jnp.arange(NK, dtype=jnp.int32)[:, None] == at_x[None]).astype(BF16)
    pick_jz = jnp.arange(NJ * NK, dtype=jnp.int32)[:, None] == at_jz[None]

    density = occupied.astype(F32) * virtual.astype(F32)
    density = density.reshape(pairs, planes, GRID, GRID)
    forward_z = jnp.concatenate([cos_k, -sin_k], axis=1)
    field = dot("pxyz,zc->pxyc", density, forward_z)
    both_y = jnp.concatenate([cos_y, sin_y], axis=1)
    mixed = dot("pxyc,yk->pxkc", field, both_y).reshape(pairs, planes, 2, PW, NJ, 2, NK)
    real = mixed[:, :, 0, :, :, 0] + mixed[:, :, 1, :, :, 1]
    imag = mixed[:, :, 0, :, :, 1] - mixed[:, :, 1, :, :, 0]
    field = jnp.stack([real, imag], axis=0).astype(BF16)
    field = field.transpose(3, 2, 1, 0, 4, 5).reshape(PW, planes, pairs * 2 * NJ * NK)
    pencil = lax.all_to_all(field, "pw", 0, 0, tiled=True).reshape(GRID, -1)

    cos_sin = jnp.concatenate([cos_k, sin_k], axis=1)
    mixed = dot("xm,xk->mk", pencil.astype(F32), cos_sin).reshape(pairs, 2, NJ * NK, 2, NK)
    real = mixed[:, 0, :, 0] + mixed[:, 1, :, 1]
    imag = mixed[:, 1, :, 0] - mixed[:, 0, :, 1]
    box = (jnp.stack([real, imag], axis=1) * (1.0 / math.sqrt(GRID**3))).astype(BF16)
    columns = jnp.einsum("prmk,mg->prkg", box, pick_jz.astype(BF16), preferred_element_type=F32)
    spectra = jnp.sum(columns * pick_x.astype(F32), axis=2).astype(BF16)

    rows = pairs * 2
    home = screened_home(spectra.reshape(rows, block), screening).astype(BF16)
    screened = home.transpose(1, 0, 2).reshape(rows, 1, block)

    spread = (screened * pick_x[None]).reshape(rows * NK, block)
    box = jnp.einsum("mg,kg->mk", pick_jz.astype(BF16), spread, preferred_element_type=F32)
    box = box.reshape(NJ * NK, rows, NK)
    mixed = dot("xk,mqk->xqm", jnp.concatenate([cos_k, sin_k], axis=0), box)
    mixed = mixed.reshape(2, GRID, pairs, 2, NJ * NK)
    real = mixed[0, :, :, 0] - mixed[1, :, :, 1]
    imag = mixed[0, :, :, 1] + mixed[1, :, :, 0]
    pencil = jnp.stack([real, imag], axis=2).astype(BF16).reshape(PW, planes, -1)
    field = lax.all_to_all(pencil, "pw", 0, 0, tiled=True)
    field = field.reshape(PW, planes, pairs, 2, NJ, NK).astype(F32)
    field = field.transpose(2, 1, 0, 4, 3, 5).reshape(pairs, planes, PW * NJ, 2 * NK)
    mixed = dot("pxkc,yk->pxyc", field, jnp.concatenate([cos_y, sin_y], axis=0))
    mixed = mixed.reshape(pairs, planes, 2, GRID, 2 * NK)
    mixed = jnp.concatenate([mixed[:, :, 0], mixed[:, :, 1]], axis=-1)
    cz, sz = jnp.transpose(cos_k), jnp.transpose(sin_k)
    back = jnp.concatenate([cz, -sz, -sz, -cz], axis=0) * (1.0 / math.sqrt(NG))
    potential = dot("pxyc,cz->pxyz", mixed, back)
    weighted = potential.reshape(pairs, planes, GRID * GRID) * occupied.astype(F32)
    return jnp.sum(weighted, axis=0)[None]


def solution(mesh):
    return jax.shard_map(
        body,
        mesh=mesh,
        in_specs=(P(None, "pw", None), P("band", "pw", None), P("pw", "band"), P()),
        out_specs=P("band", "pw", None),
        check_vma=False,
    )
```

```python
import math

import jax
import jax.numpy as jnp
from jax import lax
from jax.experimental import pallas as pl
from jax.experimental.pallas import tpu as pltpu
from jax.sharding import PartitionSpec as P

GRID = 64
NG = 16384
KMAX = 16
NK = 2 * KMAX + 1
PW = 8
BAND = 64
NJ = 5
PRECISE = lax.Precision.HIGHEST
F32 = jnp.float32
BF16 = jnp.bfloat16


def phases(left, right):
    angles = (left[:, None] * right[None, :] % GRID).astype(F32) * (2.0 * math.pi / GRID)
    return jnp.cos(angles), jnp.sin(angles)


def dot(spec, a, b):
    return jnp.einsum(spec, a, b, precision=PRECISE, preferred_element_type=F32)


MESH = pl.DeviceIdType.MESH


def remote(src, dst, send, recv, device):
    return pltpu.make_async_remote_copy(
        src_ref=src, dst_ref=dst, send_sem=send, recv_sem=recv, device_id=device, device_id_type=MESH
    )


OFFSETS = (1, 7, 2, 6, 3, 5, 4)


def screen_kernel(
    own_ref, screening_ref, home_ref, all_ref, part_ref, landed, summed, own_sem, z_sems, ys_sems,
    yr_sems, xs_sems, xr_sems, fs_sems, fr_sems, ps_sems, pr_sems, cs_sems, cr_sems
):
    band, pw = lax.axis_index("band"), lax.axis_index("pw")
    x, y, z = band // 16, lax.rem(band // 2, 8), lax.rem(band, 2)

    def at(x_at, y_at, z_at):
        return (x_at * 16 + y_at * 2 + z_at, pw)

    def up(d):
        return lax.rem(y + d, 8)

    right, left = lax.rem(x + 1, 4), lax.rem(x + 3, 4)
    across = at(x, y, 1 - z)
    beside = (at(right, y, z), at(left, y, z))
    high, low = band // PW, lax.rem(band, PW)
    same = high == pw

    def over(d):
        return lax.rem(pw + d, PW)

    barrier = pltpu.get_barrier_semaphore()
    for t in range(PW):
        @pl.when(jnp.logical_not(same & (low == t)))
        def _():
            pl.semaphore_signal(barrier, inc=1, device_id=(pw * PW + t, high), device_id_type=MESH)
    near = [across, *beside, *[at(x, up(d), z) for d in OFFSETS], *[(band, over(d)) for d in range(1, PW)]]
    for device in near:
        pl.semaphore_signal(barrier, inc=1, device_id=device, device_id_type=MESH)
    pl.semaphore_wait(barrier, len(near) + PW - jnp.where(same, 1, 0))

    keep = pltpu.make_async_copy(own_ref, all_ref.at[x, y, z], own_sem)
    keep.start()
    to_across = remote(own_ref, all_ref.at[x, y, z], z_sems.at[0], z_sems.at[1], across)
    to_across.start()
    y_copies = {}
    for d in OFFSETS:
        y_copies[0, d] = remote(
            own_ref, all_ref.at[x, y, z], ys_sems.at[0, d], yr_sems.at[0, d], at(x, up(d), z)
        )
        y_copies[0, d].start()
    to_across.wait_recv()
    other = all_ref.at[x, y, 1 - z]
    for d in OFFSETS:
        y_copies[1, d] = remote(other, other, ys_sems.at[1, d], yr_sems.at[1, d], at(x, up(d), z))
        y_copies[1, d].start()
    keep.wait()
    order = (0,) + OFFSETS
    x_copies = []
    for k, d in enumerate(order):
        if d:
            y_copies[0, d].wait_recv()
            y_copies[1, d].wait_recv()
        piece = all_ref.at[x, lax.rem(y + 8 - d, 8)]
        for side in range(2):
            copy = remote(piece, piece, xs_sems.at[side, k], xr_sems.at[side, k], beside[side])
            copy.start()
            x_copies.append(copy)
    forwards = []
    for k, d in enumerate(order):
        first = k % 2
        for side in (first, 1 - first):
            x_copies[2 * k + side].wait_recv()
            if side == first:
                source = left if side == 0 else right
                piece = all_ref.at[source, lax.rem(y + 8 - d, 8)]
                copy = remote(piece, piece, fs_sems.at[k], fr_sems.at[k], beside[side])
                copy.start()
                forwards.append(copy)
    for copy in forwards:
        copy.wait_recv()
    rows = all_ref.shape[3]
    everyone = all_ref[...].reshape(BAND * rows, all_ref.shape[4])
    partial = jnp.dot(everyone, screening_ref[...], preferred_element_type=F32).astype(BF16)
    part_ref[...] = partial.reshape(part_ref.shape)

    copies = []
    for d in range(1, PW):
        copy = remote(part_ref.at[over(d)], landed.at[pw], ps_sems.at[d], pr_sems.at[d], (band, over(d)))
        copy.start()
        copies.append(copy)
    total = part_ref[pw].astype(F32)
    for d in range(1, PW):
        copies[d - 1].wait_recv()
        total = total + landed[lax.rem(pw + PW - d, PW)].astype(F32)
    for t in range(PW):
        summed[t] = total[t * rows : (t + 1) * rows]

    def send_home(t, sem):
        return remote(summed.at[t], home_ref.at[low], cs_sems.at[t], cr_sems.at[sem], (pw * PW + t, high))

    for t in range(PW):
        mine = same & (low == t)

        @pl.when(mine)
        def _():
            own = pltpu.make_async_copy(summed.at[t], home_ref.at[low], own_sem)
            own.start()
            own.wait()

        @pl.when(jnp.logical_not(mine))
        def _():
            send_home(t, low).start()

    for t in range(PW):
        @pl.when(jnp.logical_not(same & (low == t)))
        def _():
            pltpu.make_async_remote_copy(
                src_ref=summed.at[t], dst_ref=home_ref.at[t], send_sem=cs_sems.at[t],
                recv_sem=cr_sems.at[t], device_id=(pw * PW + t, high), device_id_type=MESH,
            ).wait()
    for copy in copies:
        copy.wait_send()
    to_across.wait_send()
    for copy in [*y_copies.values(), *x_copies, *forwards]:
        copy.wait_send()


def screened_home(own, screening):
    dma = pltpu.SemaphoreType.DMA
    rows, width = own.shape[0], screening.shape[1]
    return pl.pallas_call(
        screen_kernel,
        out_shape=jax.ShapeDtypeStruct((PW, rows, width), F32),
        in_specs=[pl.BlockSpec(memory_space=pltpu.VMEM)] * 2,
        out_specs=pl.BlockSpec(memory_space=pltpu.VMEM),
        scratch_shapes=[
            pltpu.VMEM((4, 8, 2, *own.shape), BF16),
            pltpu.VMEM((PW, PW * rows, width), BF16),
            pltpu.VMEM((PW, PW * rows, width), BF16),
            pltpu.VMEM((PW, rows, width), F32),
            dma, dma((2,)), dma((2, 8)), dma((2, 8)), dma((2, 8)), dma((2, 8)), dma((8,)), dma((8,)),
            dma((PW,)), dma((PW,)), dma((PW,)), dma((PW,)),
        ],
        compiler_params=pltpu.CompilerParams(collective_id=0, has_side_effects=True),
    )(own, screening)


def exchange_kernel(from_ref, to_ref, own_sem, s_sems, r_sems):
    band, pw = lax.axis_index("band"), lax.axis_index("pw")

    def over(d):
        return lax.rem(pw + d, PW)

    barrier = pltpu.get_barrier_semaphore()
    for d in range(1, PW):
        pl.semaphore_signal(barrier, inc=1, device_id=(band, over(d)), device_id_type=MESH)
    own = pltpu.make_async_copy(from_ref.at[pw], to_ref.at[pw], own_sem)
    own.start()
    pl.semaphore_wait(barrier, PW - 1)
    copies = []
    for d in range(1, PW):
        copy = remote(from_ref.at[over(d)], to_ref.at[pw], s_sems.at[d], r_sems.at[d], (band, over(d)))
        copy.start()
        copies.append(copy)
    own.wait()
    for copy in copies:
        copy.wait()


def exchanged(blocks, collective_id):
    dma = pltpu.SemaphoreType.DMA
    return pl.pallas_call(
        exchange_kernel,
        out_shape=jax.ShapeDtypeStruct(blocks.shape, blocks.dtype),
        in_specs=[pl.BlockSpec(memory_space=pltpu.VMEM)],
        out_specs=pl.BlockSpec(memory_space=pltpu.VMEM),
        scratch_shapes=[dma, dma((PW,)), dma((PW,))],
        compiler_params=pltpu.CompilerParams(collective_id=collective_id, has_side_effects=True),
    )(blocks)


def body(occupied, virtual, screening, grid_index):
    pairs, planes = occupied.shape[0], occupied.shape[1]
    slab = lax.axis_index("pw")
    cells = jnp.arange(GRID, dtype=jnp.int32)
    freqs = jnp.arange(NK, dtype=jnp.int32) - KMAX
    row_freqs = jnp.arange(PW, dtype=jnp.int32)[:, None] - KMAX + PW * jnp.arange(NJ, dtype=jnp.int32)[None]
    cos_k, sin_k = phases(cells, freqs)
    cos_y, sin_y = phases(cells, row_freqs.reshape(-1))

    block = NG // PW
    own = lax.dynamic_slice_in_dim(grid_index, slab * block, block)

    def signed(k):
        return jnp.where(k >= GRID // 2, k - GRID, k)

    at_x = signed(own // (GRID * GRID)) + KMAX
    at_j = (signed(own // GRID % GRID) + KMAX - slab) // PW
    at_z = signed(own % GRID) + KMAX
    at_jz = at_j * NK + at_z
    pick_x = (jnp.arange(NK, dtype=jnp.int32)[:, None] == at_x[None]).astype(BF16)
    pick_jz = jnp.arange(NJ * NK, dtype=jnp.int32)[:, None] == at_jz[None]

    c = cos_y.reshape(GRID, PW, 1, NJ)
    n = sin_y.reshape(GRID, PW, 1, NJ)
    to_rows = jnp.concatenate(
        [jnp.concatenate([c, -n], axis=2), jnp.concatenate([n, c], axis=2)], axis=0
    ).reshape(2 * GRID, PW * 2 * NJ)

    occ = occupied.reshape(pairs, planes, GRID, GRID).astype(F32)
    density = occ * virtual.reshape(1, planes, GRID, GRID).astype(F32)
    field = jnp.concatenate(
        [dot("pxyz,zc->pxyc", density, cos_k), dot("pxyz,zc->pxyc", density, -sin_k)], axis=2
    )
    field = dot("yk,pxyc->pxkc", to_rows, field).astype(BF16)
    field = field.reshape(pairs, planes, PW, 2 * NJ, NK).transpose(2, 1, 0, 3, 4)
    pencil = exchanged(field.reshape(PW, planes, pairs * 2 * NJ * NK), 1).reshape(GRID, -1)

    cos_sin = jnp.concatenate([cos_k, sin_k], axis=1)
    mixed = dot("xm,xk->mk", pencil.astype(F32), cos_sin).reshape(pairs, 2, NJ * NK, 2, NK)
    real = mixed[:, 0, :, 0] + mixed[:, 1, :, 1]
    imag = mixed[:, 1, :, 0] - mixed[:, 0, :, 1]
    box = (jnp.stack([real, imag], axis=1) * (1.0 / math.sqrt(GRID**3))).astype(BF16)
    columns = jnp.einsum("prmk,mg->prkg", box, pick_jz.astype(BF16), preferred_element_type=F32)
    spectra = jnp.sum(columns * pick_x.astype(F32), axis=2).astype(BF16)

    rows = pairs * 2
    home = screened_home(spectra.reshape(rows, block), screening).astype(BF16)
    screened = home.transpose(1, 0, 2).reshape(rows, 1, block)

    spread = (screened * pick_x[None]).reshape(rows * NK, block)
    box = jnp.einsum("mg,kg->mk", pick_jz.astype(BF16), spread, preferred_element_type=F32)
    box = box.reshape(NJ * NK, rows, NK)
    mixed = dot("xk,mqk->xqm", jnp.concatenate([cos_k, sin_k], axis=0), box)
    mixed = mixed.reshape(2, GRID, pairs, 2, NJ * NK)
    real = mixed[0, :, :, 0] - mixed[1, :, :, 1]
    imag = mixed[0, :, :, 1] + mixed[1, :, :, 0]
    pencil = jnp.stack([real, imag], axis=2).astype(BF16).reshape(PW, planes, -1)
    field = exchanged(pencil, 2).reshape(PW, planes, pairs, 2 * NJ, NK)
    field = field.transpose(2, 1, 0, 3, 4).reshape(pairs, planes, PW * 2 * NJ, NK).astype(F32)
    mixed = dot("yk,pxkc->pxyc", to_rows, field)
    norm_out = 1.0 / math.sqrt(NG)
    potential = dot("pxyc,zc->pxyz", mixed[:, :, :GRID], cos_k * norm_out)
    potential = potential - dot("pxyc,zc->pxyz", mixed[:, :, GRID:], sin_k * norm_out)
    return jnp.sum(potential * occ, axis=0).reshape(1, planes, GRID * GRID)


def solution(mesh):
    return jax.shard_map(
        body,
        mesh=mesh,
        in_specs=(P(None, "pw", None), P("band", "pw", None), P("pw", "band"), P()),
        out_specs=P("band", "pw", None),
        check_vma=False,
    )
```

```python
import math

import jax
import jax.numpy as jnp
from jax import lax
from jax.experimental import pallas as pl
from jax.experimental.pallas import tpu as pltpu
from jax.sharding import PartitionSpec as P

GRID = 64
NG = 16384
KMAX = 16
NK = 2 * KMAX + 1
PW = 8
BAND = 64
NJ = 5
PRECISE = lax.Precision.HIGHEST
F32 = jnp.float32
BF16 = jnp.bfloat16


def phases(left, right):
    angles = (left[:, None] * right[None, :] % GRID).astype(F32) * (2.0 * math.pi / GRID)
    return jnp.cos(angles), jnp.sin(angles)


def dot(spec, a, b):
    return jnp.einsum(spec, a, b, precision=PRECISE, preferred_element_type=F32)


MESH = pl.DeviceIdType.MESH


def remote(src, dst, send, recv, device):
    return pltpu.make_async_remote_copy(
        src_ref=src, dst_ref=dst, send_sem=send, recv_sem=recv, device_id=device, device_id_type=MESH
    )


OFFSETS = (1, 7, 2, 6, 3, 5, 4)


def screen_kernel(
    own_ref, screening_ref, home_ref, all_ref, part_ref, landed, summed, own_sem, z_sems, ys_sems,
    yr_sems, xs_sems, xr_sems, fs_sems, fr_sems, ps_sems, pr_sems, cs_sems, cr_sems
):
    band, pw = lax.axis_index("band"), lax.axis_index("pw")
    x, y, z = band // 16, lax.rem(band // 2, 8), lax.rem(band, 2)

    def at(x_at, y_at, z_at):
        return (x_at * 16 + y_at * 2 + z_at, pw)

    def up(d):
        return lax.rem(y + d, 8)

    right, left = lax.rem(x + 1, 4), lax.rem(x + 3, 4)
    across = at(x, y, 1 - z)
    beside = (at(right, y, z), at(left, y, z))
    high, low = band // PW, lax.rem(band, PW)
    same = high == pw

    def over(d):
        return lax.rem(pw + d, PW)

    barrier = pltpu.get_barrier_semaphore()
    for t in range(PW):
        @pl.when(jnp.logical_not(same & (low == t)))
        def _():
            pl.semaphore_signal(barrier, inc=1, device_id=(pw * PW + t, high), device_id_type=MESH)
    near = [across, *beside, *[at(x, up(d), z) for d in OFFSETS], *[(band, over(d)) for d in range(1, PW)]]
    for device in near:
        pl.semaphore_signal(barrier, inc=1, device_id=device, device_id_type=MESH)
    pl.semaphore_wait(barrier, len(near) + PW - jnp.where(same, 1, 0))

    keep = pltpu.make_async_copy(own_ref, all_ref.at[x, y, z], own_sem)
    keep.start()
    to_across = remote(own_ref, all_ref.at[x, y, z], z_sems.at[0], z_sems.at[1], across)
    to_across.start()
    order = (0,) + OFFSETS
    layers = (z, 1 - z)
    y_copies, x_copies, forwards = {}, {}, {}

    def along_y(h, source):
        for d in OFFSETS:
            copy = remote(
                source, all_ref.at[x, y, layers[h]], ys_sems.at[h, d], yr_sems.at[h, d], at(x, up(d), z)
            )
            copy.start()
            y_copies[h, d] = copy

    def along_x(h, k):
        d = order[k]
        if d:
            y_copies[h, d].wait_recv()
        piece = all_ref.at[x, lax.rem(y + 8 - d, 8), layers[h]]
        for side in range(2):
            copy = remote(piece, piece, xs_sems.at[h, side, k], xr_sems.at[h, side, k], beside[side])
            copy.start()
            x_copies[h, side, k] = copy

    def onward(h, k):
        side = k % 2
        x_copies[h, side, k].wait_recv()
        piece = all_ref.at[right if side else left, lax.rem(y + 8 - order[k], 8), layers[h]]
        copy = remote(piece, piece, fs_sems.at[h, k], fr_sems.at[h, k], beside[side])
        copy.start()
        forwards[h, k] = copy

    along_y(0, own_ref)
    keep.wait()
    for k in range(5):
        along_x(0, k)
    to_across.wait_recv()
    along_y(1, all_ref.at[x, y, 1 - z])
    along_x(1, 0)
    for k in range(5, 8):
        along_x(0, k)
    onward(0, 0)
    for k in range(1, 8):
        along_x(1, k)
        onward(0, k)
    for k in range(8):
        onward(1, k)
    for h in range(2):
        for k in range(8):
            x_copies[h, 1 - k % 2, k].wait_recv()
            forwards[h, k].wait_recv()
    rows = all_ref.shape[3]
    everyone = all_ref[...].reshape(BAND * rows, all_ref.shape[4])
    partial = jnp.dot(everyone, screening_ref[...], preferred_element_type=F32).astype(BF16)
    part_ref[...] = partial.reshape(part_ref.shape)

    copies = []
    for d in range(1, PW):
        copy = remote(part_ref.at[over(d)], landed.at[pw], ps_sems.at[d], pr_sems.at[d], (band, over(d)))
        copy.start()
        copies.append(copy)
    total = part_ref[pw].astype(F32)
    for d in range(1, PW):
        copies[d - 1].wait_recv()
        total = total + landed[lax.rem(pw + PW - d, PW)].astype(F32)
    for t in range(PW):
        summed[t] = total[t * rows : (t + 1) * rows]

    def send_home(t, sem):
        return remote(summed.at[t], home_ref.at[low], cs_sems.at[t], cr_sems.at[sem], (pw * PW + t, high))

    for t in range(PW):
        mine = same & (low == t)

        @pl.when(mine)
        def _():
            own = pltpu.make_async_copy(summed.at[t], home_ref.at[low], own_sem)
            own.start()
            own.wait()

        @pl.when(jnp.logical_not(mine))
        def _():
            send_home(t, low).start()

    for t in range(PW):
        @pl.when(jnp.logical_not(same & (low == t)))
        def _():
            pltpu.make_async_remote_copy(
                src_ref=summed.at[t], dst_ref=home_ref.at[t], send_sem=cs_sems.at[t],
                recv_sem=cr_sems.at[t], device_id=(pw * PW + t, high), device_id_type=MESH,
            ).wait()
    for copy in copies:
        copy.wait_send()
    to_across.wait_send()
    for copy in [*y_copies.values(), *x_copies.values(), *forwards.values()]:
        copy.wait_send()


def screened_home(own, screening):
    dma = pltpu.SemaphoreType.DMA
    rows, width = own.shape[0], screening.shape[1]
    return pl.pallas_call(
        screen_kernel,
        out_shape=jax.ShapeDtypeStruct((PW, rows, width), F32),
        in_specs=[pl.BlockSpec(memory_space=pltpu.VMEM)] * 2,
        out_specs=pl.BlockSpec(memory_space=pltpu.VMEM),
        scratch_shapes=[
            pltpu.VMEM((4, 8, 2, *own.shape), BF16),
            pltpu.VMEM((PW, PW * rows, width), BF16),
            pltpu.VMEM((PW, PW * rows, width), BF16),
            pltpu.VMEM((PW, rows, width), F32),
            dma, dma((2,)), dma((2, 8)), dma((2, 8)), dma((2, 2, 8)), dma((2, 2, 8)), dma((2, 8)), dma((2, 8)),
            dma((PW,)), dma((PW,)), dma((PW,)), dma((PW,)),
        ],
        compiler_params=pltpu.CompilerParams(collective_id=0, has_side_effects=True),
    )(own, screening)


def body(occupied, virtual, screening, grid_index):
    pairs, planes = occupied.shape[0], occupied.shape[1]
    slab = lax.axis_index("pw")
    cells = jnp.arange(GRID, dtype=jnp.int32)
    freqs = jnp.arange(NK, dtype=jnp.int32) - KMAX
    row_freqs = jnp.arange(PW, dtype=jnp.int32)[:, None] - KMAX + PW * jnp.arange(NJ, dtype=jnp.int32)[None]
    cos_k, sin_k = phases(cells, freqs)
    cos_y, sin_y = phases(cells, row_freqs.reshape(-1))

    block = NG // PW
    own = lax.dynamic_slice_in_dim(grid_index, slab * block, block)

    def signed(k):
        return jnp.where(k >= GRID // 2, k - GRID, k)

    at_x = signed(own // (GRID * GRID)) + KMAX
    at_j = (signed(own // GRID % GRID) + KMAX - slab) // PW
    at_z = signed(own % GRID) + KMAX
    at_jz = at_j * NK + at_z
    pick_x = (jnp.arange(NK, dtype=jnp.int32)[:, None] == at_x[None]).astype(BF16)
    pick_jz = jnp.arange(NJ * NK, dtype=jnp.int32)[:, None] == at_jz[None]

    c = cos_y.reshape(GRID, PW, 1, NJ)
    n = sin_y.reshape(GRID, PW, 1, NJ)
    to_rows = jnp.concatenate(
        [jnp.concatenate([c, -n], axis=2), jnp.concatenate([n, c], axis=2)], axis=0
    ).reshape(2 * GRID, PW * 2 * NJ)

    occ = occupied.reshape(pairs, planes, GRID, GRID).astype(F32)
    density = occ * virtual.reshape(1, planes, GRID, GRID).astype(F32)
    field = dot("pxyz,zc->pxyc", density, jnp.concatenate([cos_k, -sin_k], axis=1))
    field = jnp.concatenate([field[..., :NK], field[..., NK:]], axis=2)
    field = dot("yk,pxyc->pxkc", to_rows, field).astype(BF16)
    field = field.reshape(pairs, planes, PW, 2 * NJ, NK).transpose(2, 1, 0, 3, 4)
    pencil = lax.all_to_all(
        field.reshape(PW, planes, pairs * 2 * NJ * NK), "pw", 0, 0, tiled=True
    ).reshape(GRID, -1)

    cos_sin = jnp.concatenate([cos_k, sin_k], axis=1)
    mixed = dot("xm,xk->mk", pencil.astype(F32), cos_sin).reshape(pairs, 2, NJ * NK, 2, NK)
    real = mixed[:, 0, :, 0] + mixed[:, 1, :, 1]
    imag = mixed[:, 1, :, 0] - mixed[:, 0, :, 1]
    box = (jnp.stack([real, imag], axis=1) * (1.0 / math.sqrt(GRID**3))).astype(BF16)
    columns = jnp.einsum("prmk,mg->prkg", box, pick_jz.astype(BF16), preferred_element_type=F32)
    spectra = jnp.sum(columns * pick_x.astype(F32), axis=2).astype(BF16)

    rows = pairs * 2
    home = screened_home(spectra.reshape(rows, block), screening).astype(BF16)
    screened = home.transpose(1, 0, 2).reshape(rows, 1, block)

    spread = (screened * pick_x[None]).reshape(rows * NK, block)
    box = jnp.einsum("mg,kg->mk", pick_jz.astype(BF16), spread, preferred_element_type=F32)
    box = box.reshape(NJ * NK, rows, NK)
    mixed = dot("xk,mqk->xqm", jnp.concatenate([cos_k, sin_k], axis=0), box)
    mixed = mixed.reshape(2, GRID, pairs, 2, NJ * NK)
    real = mixed[0, :, :, 0] - mixed[1, :, :, 1]
    imag = mixed[0, :, :, 1] + mixed[1, :, :, 0]
    pencil = jnp.stack([real, imag], axis=2).astype(BF16).reshape(PW, planes, -1)
    field = lax.all_to_all(pencil, "pw", 0, 0, tiled=True).reshape(PW, planes, pairs, 2 * NJ, NK)
    field = field.transpose(2, 1, 0, 3, 4).reshape(pairs, planes, PW * 2 * NJ, NK).astype(F32)
    mixed = dot("yk,pxkc->pxyc", to_rows, field)
    norm_out = 1.0 / math.sqrt(NG)
    potential = dot("pxyc,zc->pxyz", mixed[:, :, :GRID], cos_k * norm_out)
    potential = potential - dot("pxyc,zc->pxyz", mixed[:, :, GRID:], sin_k * norm_out)
    return jnp.sum(potential * occ, axis=0).reshape(1, planes, GRID * GRID)


def solution(mesh):
    return jax.shard_map(
        body,
        mesh=mesh,
        in_specs=(P(None, "pw", None), P("band", "pw", None), P("pw", "band"), P()),
        out_specs=P("band", "pw", None),
        check_vma=False,
    )
```

```python
import math

import jax
import jax.numpy as jnp
from jax import lax
from jax.experimental import pallas as pl
from jax.experimental.pallas import tpu as pltpu
from jax.sharding import PartitionSpec as P

GRID = 64
NG = 16384
KMAX = 16
NK = 2 * KMAX + 1
PW = 8
BAND = 64
NJ = 5
PRECISE = lax.Precision.HIGHEST
F32 = jnp.float32
BF16 = jnp.bfloat16


def phases(left, right):
    angles = (left[:, None] * right[None, :] % GRID).astype(F32) * (2.0 * math.pi / GRID)
    return jnp.cos(angles), jnp.sin(angles)


def dot(spec, a, b):
    return jnp.einsum(spec, a, b, precision=PRECISE, preferred_element_type=F32)


MESH = pl.DeviceIdType.MESH


def remote(src, dst, send, recv, device):
    return pltpu.make_async_remote_copy(
        src_ref=src, dst_ref=dst, send_sem=send, recv_sem=recv, device_id=device, device_id_type=MESH
    )


OFFSETS = (1, 7, 2, 6, 3, 5, 4)


def screen_kernel(
    own_ref, screening_ref, home_ref, all_ref, part_ref, landed, summed, own_sem, z_sems, ys_sems,
    yr_sems, xs_sems, xr_sems, fs_sems, fr_sems, ps_sems, pr_sems, cs_sems, cr_sems
):
    band, pw = lax.axis_index("band"), lax.axis_index("pw")
    x, y, z = band // 16, lax.rem(band // 2, 8), lax.rem(band, 2)

    def at(x_at, y_at, z_at):
        return (x_at * 16 + y_at * 2 + z_at, pw)

    def up(d):
        return lax.rem(y + d, 8)

    right, left = lax.rem(x + 1, 4), lax.rem(x + 3, 4)
    across = at(x, y, 1 - z)
    beside = (at(right, y, z), at(left, y, z))
    high, low = band // PW, lax.rem(band, PW)
    same = high == pw

    def over(d):
        return lax.rem(pw + d, PW)

    barrier = pltpu.get_barrier_semaphore()
    for t in range(PW):
        @pl.when(jnp.logical_not(same & (low == t)))
        def _():
            pl.semaphore_signal(barrier, inc=1, device_id=(pw * PW + t, high), device_id_type=MESH)
    near = [across, *beside, *[at(x, up(d), z) for d in OFFSETS], *[(band, over(d)) for d in range(1, PW)]]
    for device in near:
        pl.semaphore_signal(barrier, inc=1, device_id=device, device_id_type=MESH)
    pl.semaphore_wait(barrier, len(near) + PW - jnp.where(same, 1, 0))

    keep = pltpu.make_async_copy(own_ref, all_ref.at[x, y, z], own_sem)
    keep.start()
    to_across = remote(own_ref, all_ref.at[x, y, z], z_sems.at[0], z_sems.at[1], across)
    to_across.start()
    order = (0,) + OFFSETS
    layers = (z, 1 - z)
    y_copies, x_copies, forwards = {}, {}, {}

    def along_y(h, source):
        for d in OFFSETS:
            copy = remote(
                source, all_ref.at[x, y, layers[h]], ys_sems.at[h, d], yr_sems.at[h, d], at(x, up(d), z)
            )
            copy.start()
            y_copies[h, d] = copy

    def along_x(h, k):
        d = order[k]
        if d:
            y_copies[h, d].wait_recv()
        piece = all_ref.at[x, lax.rem(y + 8 - d, 8), layers[h]]
        for side in range(2):
            copy = remote(piece, piece, xs_sems.at[h, side, k], xr_sems.at[h, side, k], beside[side])
            copy.start()
            x_copies[h, side, k] = copy

    def onward(h, k):
        side = k % 2
        x_copies[h, side, k].wait_recv()
        piece = all_ref.at[right if side else left, lax.rem(y + 8 - order[k], 8), layers[h]]
        copy = remote(piece, piece, fs_sems.at[h, k], fr_sems.at[h, k], beside[side])
        copy.start()
        forwards[h, k] = copy

    along_y(0, own_ref)
    keep.wait()
    for k in range(5):
        along_x(0, k)
    to_across.wait_recv()
    along_y(1, all_ref.at[x, y, 1 - z])
    along_x(1, 0)
    for k in range(5, 8):
        along_x(0, k)
    onward(0, 0)
    for k in range(1, 8):
        along_x(1, k)
        onward(0, k)
    for k in range(8):
        onward(1, k)
    rows = all_ref.shape[3]

    def part_send(q):
        d = lax.rem(q - pw + PW, PW)
        return remote(part_ref.at[q], landed.at[pw], ps_sems.at[d], pr_sems.at[d], (band, q))

    def screen(x_at):
        block = all_ref[x_at].reshape(16 * rows, all_ref.shape[4])
        product = jnp.dot(block, screening_ref[...], preferred_element_type=F32).astype(BF16)
        part_ref[pl.ds(2 * x_at, 2)] = product.reshape(2, PW * rows, product.shape[1])
        for e in range(2):
            q = 2 * x_at + e

            @pl.when(q != pw)
            def _():
                part_send(q).start()

    screen(x)
    for side in (1, 0):
        for h in range(2):
            for k in range(8):
                if k % 2 != side:
                    x_copies[h, side, k].wait_recv()
        screen(right if side else left)
    for copy in forwards.values():
        copy.wait_recv()
    screen(lax.rem(x + 2, 4))

    copies = [part_send(over(d)) for d in range(1, PW)]
    total = part_ref[pw].astype(F32)
    for d in range(1, PW):
        copies[d - 1].wait_recv()
        total = total + landed[lax.rem(pw + PW - d, PW)].astype(F32)
    for t in range(PW):
        summed[t] = total[t * rows : (t + 1) * rows]

    def send_home(t, sem):
        return remote(summed.at[t], home_ref.at[low], cs_sems.at[t], cr_sems.at[sem], (pw * PW + t, high))

    for t in range(PW):
        mine = same & (low == t)

        @pl.when(mine)
        def _():
            own = pltpu.make_async_copy(summed.at[t], home_ref.at[low], own_sem)
            own.start()
            own.wait()

        @pl.when(jnp.logical_not(mine))
        def _():
            send_home(t, low).start()

    for t in range(PW):
        @pl.when(jnp.logical_not(same & (low == t)))
        def _():
            pltpu.make_async_remote_copy(
                src_ref=summed.at[t], dst_ref=home_ref.at[t], send_sem=cs_sems.at[t],
                recv_sem=cr_sems.at[t], device_id=(pw * PW + t, high), device_id_type=MESH,
            ).wait()
    for copy in copies:
        copy.wait_send()
    to_across.wait_send()
    for copy in [*y_copies.values(), *x_copies.values(), *forwards.values()]:
        copy.wait_send()


def screened_home(own, screening):
    dma = pltpu.SemaphoreType.DMA
    rows, width = own.shape[0], screening.shape[1]
    return pl.pallas_call(
        screen_kernel,
        out_shape=jax.ShapeDtypeStruct((PW, rows, width), F32),
        in_specs=[pl.BlockSpec(memory_space=pltpu.VMEM)] * 2,
        out_specs=pl.BlockSpec(memory_space=pltpu.VMEM),
        scratch_shapes=[
            pltpu.VMEM((4, 8, 2, *own.shape), BF16),
            pltpu.VMEM((PW, PW * rows, width), BF16),
            pltpu.VMEM((PW, PW * rows, width), BF16),
            pltpu.VMEM((PW, rows, width), F32),
            dma, dma((2,)), dma((2, 8)), dma((2, 8)), dma((2, 2, 8)), dma((2, 2, 8)), dma((2, 8)), dma((2, 8)),
            dma((PW,)), dma((PW,)), dma((PW,)), dma((PW,)),
        ],
        compiler_params=pltpu.CompilerParams(collective_id=0, has_side_effects=True),
    )(own, screening)


def body(occupied, virtual, screening, grid_index):
    pairs, planes = occupied.shape[0], occupied.shape[1]
    slab = lax.axis_index("pw")
    cells = jnp.arange(GRID, dtype=jnp.int32)
    freqs = jnp.arange(NK, dtype=jnp.int32) - KMAX
    row_freqs = jnp.arange(PW, dtype=jnp.int32)[:, None] - KMAX + PW * jnp.arange(NJ, dtype=jnp.int32)[None]
    cos_k, sin_k = phases(cells, freqs)
    cos_y, sin_y = phases(cells, row_freqs.reshape(-1))

    block = NG // PW
    own = lax.dynamic_slice_in_dim(grid_index, slab * block, block)

    def signed(k):
        return jnp.where(k >= GRID // 2, k - GRID, k)

    at_x = signed(own // (GRID * GRID)) + KMAX
    at_j = (signed(own // GRID % GRID) + KMAX - slab) // PW
    at_z = signed(own % GRID) + KMAX
    at_jz = at_j * NK + at_z
    pick_x = (jnp.arange(NK, dtype=jnp.int32)[:, None] == at_x[None]).astype(BF16)
    pick_jz = jnp.arange(NJ * NK, dtype=jnp.int32)[:, None] == at_jz[None]

    c = cos_y.reshape(GRID, PW, 1, NJ)
    n = sin_y.reshape(GRID, PW, 1, NJ)
    to_rows = jnp.concatenate(
        [jnp.concatenate([c, -n], axis=2), jnp.concatenate([n, c], axis=2)], axis=0
    ).reshape(2 * GRID, PW * 2 * NJ)

    occ = occupied.reshape(pairs, planes, GRID, GRID).astype(F32)
    density = occ * virtual.reshape(1, planes, GRID, GRID).astype(F32)
    field = dot("pxyz,zc->pxyc", density, jnp.concatenate([cos_k, -sin_k], axis=1))
    field = jnp.concatenate([field[..., :NK], field[..., NK:]], axis=2)
    field = dot("yk,pxyc->pxkc", to_rows, field).astype(BF16)
    field = field.reshape(pairs, planes, PW, 2 * NJ, NK).transpose(2, 1, 0, 3, 4)
    pencil = lax.all_to_all(
        field.reshape(PW, planes, pairs * 2 * NJ * NK), "pw", 0, 0, tiled=True
    ).reshape(GRID, -1)

    cos_sin = jnp.concatenate([cos_k, sin_k], axis=1)
    mixed = dot("xm,xk->mk", pencil.astype(F32), cos_sin).reshape(pairs, 2, NJ * NK, 2, NK)
    real = mixed[:, 0, :, 0] + mixed[:, 1, :, 1]
    imag = mixed[:, 1, :, 0] - mixed[:, 0, :, 1]
    box = (jnp.stack([real, imag], axis=1) * (1.0 / math.sqrt(GRID**3))).astype(BF16)
    columns = jnp.einsum("prmk,mg->prkg", box, pick_jz.astype(BF16), preferred_element_type=F32)
    spectra = jnp.sum(columns * pick_x.astype(F32), axis=2).astype(BF16)

    rows = pairs * 2
    home = screened_home(spectra.reshape(rows, block), screening).astype(BF16)
    screened = home.transpose(1, 0, 2).reshape(rows, 1, block)

    spread = (screened * pick_x[None]).reshape(rows * NK, block)
    box = jnp.einsum("mg,kg->mk", pick_jz.astype(BF16), spread, preferred_element_type=F32)
    box = box.reshape(NJ * NK, rows, NK)
    mixed = dot("xk,mqk->xqm", jnp.concatenate([cos_k, sin_k], axis=0), box)
    mixed = mixed.reshape(2, GRID, pairs, 2, NJ * NK)
    real = mixed[0, :, :, 0] - mixed[1, :, :, 1]
    imag = mixed[0, :, :, 1] + mixed[1, :, :, 0]
    pencil = jnp.stack([real, imag], axis=2).astype(BF16).reshape(PW, planes, -1)
    field = lax.all_to_all(pencil, "pw", 0, 0, tiled=True).reshape(PW, planes, pairs, 2 * NJ, NK)
    field = field.transpose(2, 1, 0, 3, 4).reshape(pairs, planes, PW * 2 * NJ, NK).astype(F32)
    mixed = dot("yk,pxkc->pxyc", to_rows, field)
    norm_out = 1.0 / math.sqrt(NG)
    potential = dot("pxyc,zc->pxyz", mixed[:, :, :GRID], cos_k * norm_out)
    potential = potential - dot("pxyc,zc->pxyz", mixed[:, :, GRID:], sin_k * norm_out)
    return jnp.sum(potential * occ, axis=0).reshape(1, planes, GRID * GRID)


def solution(mesh):
    return jax.shard_map(
        body,
        mesh=mesh,
        in_specs=(P(None, "pw", None), P("band", "pw", None), P("pw", "band"), P()),
        out_specs=P("band", "pw", None),
        check_vma=False,
    )
```

```python
import math

import jax
import jax.numpy as jnp
from jax import lax
from jax.experimental import pallas as pl
from jax.experimental.pallas import tpu as pltpu
from jax.sharding import PartitionSpec as P

GRID = 64
NG = 16384
KMAX = 16
NK = 2 * KMAX + 1
PW = 8
BAND = 64
NJ = 5
PRECISE = lax.Precision.HIGH
F32 = jnp.float32
BF16 = jnp.bfloat16


def phases(left, right):
    angles = (left[:, None] * right[None, :] % GRID).astype(F32) * (2.0 * math.pi / GRID)
    return jnp.cos(angles), jnp.sin(angles)


def dot(spec, a, b):
    return jnp.einsum(spec, a, b, precision=PRECISE, preferred_element_type=F32)


MESH = pl.DeviceIdType.MESH


def remote(src, dst, send, recv, device):
    return pltpu.make_async_remote_copy(
        src_ref=src, dst_ref=dst, send_sem=send, recv_sem=recv, device_id=device, device_id_type=MESH
    )


OFFSETS = (1, 7, 2, 6, 3, 5, 4)


def screen_kernel(
    own_ref, screening_ref, home_ref, all_ref, part_ref, landed, summed, own_sem, z_sems, ys_sems,
    yr_sems, xs_sems, xr_sems, fs_sems, fr_sems, ps_sems, pr_sems, cs_sems, cr_sems
):
    band, pw = lax.axis_index("band"), lax.axis_index("pw")
    x, y, z = band // 16, lax.rem(band // 2, 8), lax.rem(band, 2)

    def at(x_at, y_at, z_at):
        return (x_at * 16 + y_at * 2 + z_at, pw)

    def up(d):
        return lax.rem(y + d, 8)

    right, left = lax.rem(x + 1, 4), lax.rem(x + 3, 4)
    across = at(x, y, 1 - z)
    beside = (at(right, y, z), at(left, y, z))
    high, low = band // PW, lax.rem(band, PW)
    same = high == pw

    def over(d):
        return lax.rem(pw + d, PW)

    barrier = pltpu.get_barrier_semaphore()
    for t in range(PW):
        @pl.when(jnp.logical_not(same & (low == t)))
        def _():
            pl.semaphore_signal(barrier, inc=1, device_id=(pw * PW + t, high), device_id_type=MESH)
    near = [across, *beside, *[at(x, up(d), z) for d in OFFSETS], *[(band, over(d)) for d in range(1, PW)]]
    for device in near:
        pl.semaphore_signal(barrier, inc=1, device_id=device, device_id_type=MESH)
    pl.semaphore_wait(barrier, len(near) + PW - jnp.where(same, 1, 0))

    keep = pltpu.make_async_copy(own_ref, all_ref.at[x, y, z], own_sem)
    keep.start()
    to_across = remote(own_ref, all_ref.at[x, y, z], z_sems.at[0], z_sems.at[1], across)
    to_across.start()
    order = (0,) + OFFSETS
    layers = (z, 1 - z)
    y_copies, x_copies, forwards = {}, {}, {}

    def along_y(h, source):
        for d in OFFSETS:
            copy = remote(
                source, all_ref.at[x, y, layers[h]], ys_sems.at[h, d], yr_sems.at[h, d], at(x, up(d), z)
            )
            copy.start()
            y_copies[h, d] = copy

    def along_x(h, k):
        d = order[k]
        if d:
            y_copies[h, d].wait_recv()
        piece = all_ref.at[x, lax.rem(y + 8 - d, 8), layers[h]]
        for side in range(2):
            copy = remote(piece, piece, xs_sems.at[h, side, k], xr_sems.at[h, side, k], beside[side])
            copy.start()
            x_copies[h, side, k] = copy

    def onward(h, k):
        side = k % 2
        x_copies[h, side, k].wait_recv()
        piece = all_ref.at[right if side else left, lax.rem(y + 8 - order[k], 8), layers[h]]
        copy = remote(piece, piece, fs_sems.at[h, k], fr_sems.at[h, k], beside[side])
        copy.start()
        forwards[h, k] = copy

    along_y(0, own_ref)
    keep.wait()
    for k in range(5):
        along_x(0, k)
    to_across.wait_recv()
    along_y(1, all_ref.at[x, y, 1 - z])
    along_x(1, 0)
    for k in range(5, 8):
        along_x(0, k)
    onward(0, 0)
    for k in range(1, 8):
        along_x(1, k)
        onward(0, k)
    for k in range(8):
        onward(1, k)
    rows = all_ref.shape[3]

    def part_send(q):
        d = lax.rem(q - pw + PW, PW)
        return remote(part_ref.at[q], landed.at[pw], ps_sems.at[d], pr_sems.at[d], (band, q))

    def screen(x_at):
        block = all_ref[x_at].reshape(16 * rows, all_ref.shape[4])
        product = jnp.dot(block, screening_ref[...], preferred_element_type=F32).astype(BF16)
        part_ref[pl.ds(2 * x_at, 2)] = product.reshape(2, PW * rows, product.shape[1])
        for e in range(2):
            q = 2 * x_at + e

            @pl.when(q != pw)
            def _():
                part_send(q).start()

    screen(x)
    for side in (1, 0):
        for h in range(2):
            for k in range(8):
                if k % 2 != side:
                    x_copies[h, side, k].wait_recv()
        screen(right if side else left)
    for copy in forwards.values():
        copy.wait_recv()
    screen(lax.rem(x + 2, 4))

    copies = [part_send(over(d)) for d in range(1, PW)]
    total = part_ref[pw].astype(F32)
    for d in range(1, PW):
        copies[d - 1].wait_recv()
        total = total + landed[lax.rem(pw + PW - d, PW)].astype(F32)
    for t in range(PW):
        summed[t] = total[t * rows : (t + 1) * rows]

    def send_home(t, sem):
        return remote(summed.at[t], home_ref.at[low], cs_sems.at[t], cr_sems.at[sem], (pw * PW + t, high))

    for t in range(PW):
        mine = same & (low == t)

        @pl.when(mine)
        def _():
            own = pltpu.make_async_copy(summed.at[t], home_ref.at[low], own_sem)
            own.start()
            own.wait()

        @pl.when(jnp.logical_not(mine))
        def _():
            send_home(t, low).start()

    for t in range(PW):
        @pl.when(jnp.logical_not(same & (low == t)))
        def _():
            pltpu.make_async_remote_copy(
                src_ref=summed.at[t], dst_ref=home_ref.at[t], send_sem=cs_sems.at[t],
                recv_sem=cr_sems.at[t], device_id=(pw * PW + t, high), device_id_type=MESH,
            ).wait()
    for copy in copies:
        copy.wait_send()
    to_across.wait_send()
    for copy in [*y_copies.values(), *x_copies.values(), *forwards.values()]:
        copy.wait_send()


def screened_home(own, screening):
    dma = pltpu.SemaphoreType.DMA
    rows, width = own.shape[0], screening.shape[1]
    return pl.pallas_call(
        screen_kernel,
        out_shape=jax.ShapeDtypeStruct((PW, rows, width), F32),
        in_specs=[pl.BlockSpec(memory_space=pltpu.VMEM)] * 2,
        out_specs=pl.BlockSpec(memory_space=pltpu.VMEM),
        scratch_shapes=[
            pltpu.VMEM((4, 8, 2, *own.shape), BF16),
            pltpu.VMEM((PW, PW * rows, width), BF16),
            pltpu.VMEM((PW, PW * rows, width), BF16),
            pltpu.VMEM((PW, rows, width), F32),
            dma, dma((2,)), dma((2, 8)), dma((2, 8)), dma((2, 2, 8)), dma((2, 2, 8)), dma((2, 8)), dma((2, 8)),
            dma((PW,)), dma((PW,)), dma((PW,)), dma((PW,)),
        ],
        compiler_params=pltpu.CompilerParams(collective_id=0, has_side_effects=True),
    )(own, screening)


def body(occupied, virtual, screening, grid_index):
    pairs, planes = occupied.shape[0], occupied.shape[1]
    slab = lax.axis_index("pw")
    cells = jnp.arange(GRID, dtype=jnp.int32)
    freqs = jnp.arange(NK, dtype=jnp.int32) - KMAX
    row_freqs = jnp.arange(PW, dtype=jnp.int32)[:, None] - KMAX + PW * jnp.arange(NJ, dtype=jnp.int32)[None]
    cos_k, sin_k = phases(cells, freqs)
    cos_y, sin_y = phases(cells, row_freqs.reshape(-1))

    block = NG // PW
    own = lax.dynamic_slice_in_dim(grid_index, slab * block, block)

    def signed(k):
        return jnp.where(k >= GRID // 2, k - GRID, k)

    at_x = signed(own // (GRID * GRID)) + KMAX
    at_j = (signed(own // GRID % GRID) + KMAX - slab) // PW
    at_z = signed(own % GRID) + KMAX
    at_jz = at_j * NK + at_z
    pick_x = (jnp.arange(NK, dtype=jnp.int32)[:, None] == at_x[None]).astype(BF16)
    pick_jz = jnp.arange(NJ * NK, dtype=jnp.int32)[:, None] == at_jz[None]

    c = cos_y.reshape(GRID, PW, 1, NJ)
    n = sin_y.reshape(GRID, PW, 1, NJ)
    to_rows = jnp.concatenate(
        [jnp.concatenate([c, -n], axis=2), jnp.concatenate([n, c], axis=2)], axis=0
    ).reshape(2 * GRID, PW * 2 * NJ)

    occ = occupied.reshape(pairs, planes, GRID, GRID).astype(F32)
    density = occ * virtual.reshape(1, planes, GRID, GRID).astype(F32)
    field = dot("pxyz,zc->pxyc", density, jnp.concatenate([cos_k, -sin_k], axis=1))
    field = jnp.concatenate([field[..., :NK], field[..., NK:]], axis=2)
    field = dot("yk,pxyc->pxkc", to_rows, field).astype(BF16)
    field = field.reshape(pairs, planes, PW, 2 * NJ, NK).transpose(2, 1, 0, 3, 4)
    pencil = lax.all_to_all(
        field.reshape(PW, planes, pairs * 2 * NJ * NK), "pw", 0, 0, tiled=True
    ).reshape(GRID, -1)

    cos_sin = jnp.concatenate([cos_k, sin_k], axis=1)
    mixed = dot("xm,xk->mk", pencil.astype(F32), cos_sin).reshape(pairs, 2, NJ * NK, 2, NK)
    real = mixed[:, 0, :, 0] + mixed[:, 1, :, 1]
    imag = mixed[:, 1, :, 0] - mixed[:, 0, :, 1]
    box = (jnp.stack([real, imag], axis=1) * (1.0 / math.sqrt(GRID**3))).astype(BF16)
    columns = jnp.einsum("prmk,mg->prkg", box, pick_jz.astype(BF16), preferred_element_type=F32)
    spectra = jnp.sum(columns * pick_x.astype(F32), axis=2).astype(BF16)

    rows = pairs * 2
    home = screened_home(spectra.reshape(rows, block), screening).astype(BF16)
    screened = home.transpose(1, 0, 2).reshape(rows, 1, block)

    spread = (screened * pick_x[None]).reshape(rows * NK, block)
    box = jnp.einsum("mg,kg->mk", pick_jz.astype(BF16), spread, preferred_element_type=F32)
    box = box.reshape(NJ * NK, rows, NK)
    mixed = dot("xk,mqk->xqm", jnp.concatenate([cos_k, sin_k], axis=0), box)
    mixed = mixed.reshape(2, GRID, pairs, 2, NJ * NK)
    real = mixed[0, :, :, 0] - mixed[1, :, :, 1]
    imag = mixed[0, :, :, 1] + mixed[1, :, :, 0]
    pencil = jnp.stack([real, imag], axis=2).astype(BF16).reshape(PW, planes, -1)
    field = lax.all_to_all(pencil, "pw", 0, 0, tiled=True).reshape(PW, planes, pairs, 2 * NJ, NK)
    field = field.transpose(2, 1, 0, 3, 4).reshape(pairs, planes, PW * 2 * NJ, NK).astype(F32)
    mixed = dot("yk,pxkc->pxyc", to_rows, field)
    norm_out = 1.0 / math.sqrt(NG)
    potential = dot("pxyc,zc->pxyz", mixed[:, :, :GRID], cos_k * norm_out)
    potential = potential - dot("pxyc,zc->pxyz", mixed[:, :, GRID:], sin_k * norm_out)
    return jnp.sum(potential * occ, axis=0).reshape(1, planes, GRID * GRID)


def solution(mesh):
    return jax.shard_map(
        body,
        mesh=mesh,
        in_specs=(P(None, "pw", None), P("band", "pw", None), P("pw", "band"), P()),
        out_specs=P("band", "pw", None),
        check_vma=False,
    )
```
